32 devices in a mesh: tok: 8 (over z, x), head: 4 (over y, core).
Axes of the slice: x: 2, y: 2, z: 4, core: 2. Of those that a mesh axis runs over, the one named last changes fastest.
Arguments:
- tri_tokens: bfloat16 [4096, 1024], P(('tok', 'head')), may hold values from -6 to 6
- image_tokens: bfloat16 [32768, 1024], P('tok'), may hold values from -6 to 6
- cross_q: bfloat16 [1024, 1024], P(None, 'head'), may hold values from -0.1875 to 0.1875
- cross_kv: bfloat16 [2, 1024, 1024], P(None, None, 'head'), may hold values from -0.1875 to 0.1875
- cross_out: bfloat16 [1024, 1024], P('head'), may hold values from -0.1875 to 0.1875
- self_qkv: bfloat16 [3, 1024, 1024], P(None, None, 'head'), may hold values from -0.1875 to 0.1875
- self_out: bfloat16 [1024, 1024], P('head'), may hold values from -0.1875 to 0.1875
- mlp_in: bfloat16 [1024, 4096], P(None, 'head'), may hold values from -0.1875 to 0.1875
- mlp_out: bfloat16 [4096, 1024], P('head'), may hold values from -0.09375 to 0.09375
Outputs:
- tri_out: bfloat16 [4096, 1024], P(('tok', 'head'))
The draws below stay inside these ranges and needn't reach their ends.
All inputs are finite; a program needn't handle non-finite values.
Results may differ from the reference program's by a relative error of at most 0.013.
Values may be sent and summed in bfloat16 or wider, within the bound.
A program may use at most 128 MiB of HBM per device.

```python
import math
import jax
import jax.numpy as jnp
from jax import lax

D = 1024
HEADS = 16
FF = 4096
TRI = 4096
IMG = 32768


def level_of(key, extent, cuts, least, top_value):
    factor_of = 1.0
    for axis_at, blocks in cuts:
        steps = jax.random.uniform(jax.random.fold_in(jax.random.fold_in(key, 6), axis_at), (blocks,), jnp.float32, least / len(cuts), top_value / len(cuts))
        factor_of = factor_of * jnp.repeat(jnp.exp(steps), extent[axis_at] // blocks).reshape((-1,) + (1,) * (len(extent) - 1 - axis_at))
    return factor_of


def scatter_about(rng, extent, deviation, reach, pieces=(), dtype=jnp.bfloat16):
    values = jax.random.normal(rng, extent, jnp.float32) * deviation
    if len(pieces) > 0:
        values = level_of(rng, extent, pieces, -0.22, 0.18) * values
    return jnp.clip(values, min=-reach, max=reach).astype(dtype)


def setup_inputs(seed: int = 0) -> dict:
    key_of = jax.random.split(jax.random.key(seed), 10)
    return {
        "tri_tokens": scatter_about(key_of[0], (TRI, D), 1.0, 6.0, ((0, 32),)),
        "image_tokens": scatter_about(key_of[1], (IMG, D), 1.0, 6.0, ((0, 8),)),
        "cross_q": scatter_about(key_of[2], (D, D), D ** -0.5, 0.1875, ((1, 4),)),
        "cross_kv": scatter_about(key_of[3], (2, D, D), D ** -0.5, 0.1875, ((2, 4),)),
        "cross_out": scatter_about(key_of[4], (D, D), D ** -0.5, 0.1875, ((0, 4),)),
        "self_qkv": scatter_about(key_of[5], (3, D, D), D ** -0.5, 0.1875, ((2, 4),)),
        "self_out": scatter_about(key_of[6], (D, D), D ** -0.5, 0.1875, ((0, 4),)),
        "mlp_in": scatter_about(key_of[7], (D, FF), D ** -0.5, 0.1875, ((1, 4),)),
        "mlp_out": scatter_about(key_of[8], (FF, D), FF ** -0.5, 0.09375, ((0, 4),)),
    }


score_gain = 2.5

def layer_norm(values):
    centered = values - lax.optimization_barrier(jnp.mean(values, axis=-1, keepdims=True))
    return centered * lax.rsqrt(lax.optimization_barrier(jnp.mean(centered * centered, axis=-1, keepdims=True)) + 1e-05)

def head_norm(values, head_count):
    shaped = values.reshape(values.shape[0], head_count, -1)
    normed = shaped * lax.rsqrt(lax.optimization_barrier(jnp.mean(shaped * shaped, axis=-1, keepdims=True)) + 1e-06)
    return normed.reshape(values.shape[0], -1).astype(jnp.bfloat16)

def partial_attention(queries, kv_rows, head_count):
    query_count = queries.shape[0]
    head_size = queries.shape[1] // head_count
    score_scale = score_gain / math.sqrt(head_size)
    query_block = math.gcd(query_count, 512)
    key_block = math.gcd(kv_rows.shape[0], 2048)
    query_blocks = queries.reshape(query_count // query_block, query_block, head_count, head_size)
    key_blocks = kv_rows.reshape(kv_rows.shape[0] // key_block, key_block, 2, head_count, head_size)

    def one_block(query_tile):

        def key_step(running, key_tile):
            weighted, totals = running
            scores = jnp.einsum('qhd,khd->qhk', query_tile, key_tile[:, 0], preferred_element_type=jnp.float32) * score_scale
            exp_scores = jnp.exp(scores)
            totals = totals + lax.optimization_barrier(jnp.sum(exp_scores, axis=-1))
            weighted = weighted + jnp.einsum('qhk,khd->qhd', exp_scores.astype(jnp.bfloat16), key_tile[:, 1], preferred_element_type=jnp.float32)
            return ((weighted, totals), None)
        starting = (jnp.zeros((query_block, head_count, head_size), jnp.float32), jnp.zeros((query_block, head_count), jnp.float32))
        result, _ = lax.scan(key_step, starting, key_blocks)
        return result
    weighted, totals = lax.map(one_block, query_blocks)
    return (weighted.reshape(query_count, head_count, head_size), totals.reshape(query_count, head_count))

def finish(weighted, totals):
    return (weighted / totals[:, :, None]).reshape(weighted.shape[0], -1).astype(jnp.bfloat16)

def reference(tri_tokens, image_tokens, cross_q, cross_kv, cross_out, self_qkv, self_out, mlp_in, mlp_out):
    stream_zero = tri_tokens.astype(jnp.float32)
    normed_one = layer_norm(stream_zero).astype(jnp.bfloat16)
    queries = head_norm(jnp.dot(normed_one, cross_q, preferred_element_type=jnp.float32), HEADS)
    kv_weight = jnp.concatenate([cross_kv[0], cross_kv[1]], axis=1)
    image_kv = jnp.dot(image_tokens, kv_weight, preferred_element_type=jnp.float32)
    view_kv = jnp.concatenate([head_norm(image_kv[:, :D], HEADS), image_kv[:, D:].astype(jnp.bfloat16)], axis=1)
    weighted, totals = partial_attention(queries, view_kv, HEADS)
    cross_mix = finish(weighted, totals)
    stream_one = stream_zero + jnp.dot(cross_mix, cross_out, preferred_element_type=jnp.float32)
    normed_two = layer_norm(stream_one).astype(jnp.bfloat16)
    self_weight = jnp.concatenate([self_qkv[0], self_qkv[1], self_qkv[2]], axis=1)
    mixed = jnp.dot(normed_two, self_weight, preferred_element_type=jnp.float32)
    self_queries = head_norm(mixed[:, :D], HEADS)
    self_kv = jnp.concatenate([head_norm(mixed[:, D:2 * D], HEADS), mixed[:, 2 * D:].astype(jnp.bfloat16)], axis=1)
    weighted, totals = partial_attention(self_queries, self_kv, HEADS)
    self_mix = finish(weighted, totals)
    stream_two = stream_one + jnp.dot(self_mix, self_out, preferred_element_type=jnp.float32)
    normed_three = layer_norm(stream_two).astype(jnp.bfloat16)
    hidden = jax.nn.gelu(jnp.dot(normed_three, mlp_in, preferred_element_type=jnp.float32), approximate=True).astype(jnp.bfloat16)
    return (stream_two + jnp.dot(hidden, mlp_out, preferred_element_type=jnp.float32)).astype(jnp.bfloat16)
```

```python
import functools
import math

import jax
import jax.numpy as jnp
from jax import lax
from jax.experimental import pallas as pl
from jax.experimental.pallas import tpu as pltpu
from jax.sharding import PartitionSpec as P

HEADS = 16
score_gain = 2.5
VMEM_LIMIT = 56 << 20


def layer_norm(values):
    centered = values - jnp.mean(values, axis=-1, keepdims=True)
    return centered * lax.rsqrt(jnp.mean(centered * centered, axis=-1, keepdims=True) + 1e-05)


def head_scale(product, head_size):
    width = product.shape[1]
    rows = lax.broadcasted_iota(jnp.int32, (width, width), 0) // head_size
    cols = lax.broadcasted_iota(jnp.int32, (width, width), 1) // head_size
    same = (rows == cols).astype(jnp.float32).astype(jnp.bfloat16)
    squares = product * product
    high = squares.astype(jnp.bfloat16)
    low = (squares - high.astype(jnp.float32)).astype(jnp.bfloat16)
    total = jnp.dot(high, same, preferred_element_type=jnp.float32)
    total = total + jnp.dot(low, same, preferred_element_type=jnp.float32)
    return lax.rsqrt(total * (1.0 / head_size) + 1e-06)


def project_kernel(x_ref, w_ref, *out_refs, plan, head_size):
    width = w_ref.shape[2]
    for j, (place, column, factor) in enumerate(plan):
        product = jnp.dot(x_ref[...], w_ref[j], preferred_element_type=jnp.float32)
        if factor is not None:
            product = product * (head_scale(product, head_size) * factor)
        out_refs[place][:, column * width : (column + 1) * width] = product.astype(jnp.bfloat16)


def project(x, weights, plan, head_size):
    rows, depth = x.shape
    count, _, width = weights.shape
    block = math.gcd(rows, 512)
    places = max(p for p, _, _ in plan) + 1
    widths = [width * sum(p == place for p, _, _ in plan) for place in range(places)]
    return pl.pallas_call(
        functools.partial(project_kernel, plan=plan, head_size=head_size),
        out_shape=[jax.ShapeDtypeStruct((rows, w), jnp.bfloat16) for w in widths],
        grid=(rows // block,),
        in_specs=[
            pl.BlockSpec((block, depth), lambda i: (i, 0)),
            pl.BlockSpec((count, depth, width), lambda i: (0, 0, 0)),
        ],
        out_specs=[pl.BlockSpec((block, w), lambda i: (i, 0)) for w in widths],
        compiler_params=pltpu.CompilerParams(vmem_limit_bytes=VMEM_LIMIT),
        cost_estimate=pl.CostEstimate(
            flops=2 * rows * depth * width * count,
            bytes_accessed=2 * (rows * depth + count * depth * width + rows * width * count),
            transcendentals=rows * width,
        ),
    )(x, weights)


def stack_heads(queries, head_size):
    rows, lanes = queries.shape
    lane = lax.broadcasted_iota(jnp.int32, (rows, lanes), 1) // head_size
    zero = jnp.zeros_like(queries)
    heads = lanes // head_size
    if heads == 1:
        return queries
    return jnp.concatenate([jnp.where(lane == h, queries, zero) for h in range(heads)], axis=0)


def pick_heads(acc_ref, rows, lanes, head_size):
    picked = acc_ref[:rows, :]
    lane = lax.broadcasted_iota(jnp.int32, picked.shape, 1) % lanes // head_size
    for h in range(1, lanes // head_size):
        picked = jnp.where(lane == h, acc_ref[h * rows : (h + 1) * rows, :], picked)
    return picked[:, :lanes], picked[:, lanes:]


def fold_keys(stacked, key_of, value_of, acc_ref, key_count, lanes):
    block = math.gcd(key_count, 512)
    ones = jnp.ones((block, lanes), jnp.bfloat16)
    acc_ref[...] = jnp.zeros_like(acc_ref)

    def step(i, carry):
        rows = pl.ds(pl.multiple_of(i * block, block), block)
        scores = lax.dot_general(
            stacked, key_of(rows), (((1,), (1,)), ((), ())), preferred_element_type=jnp.float32
        )
        weights = jnp.exp2(scores).astype(jnp.bfloat16)
        values = jnp.concatenate([value_of(rows), ones], axis=1)
        acc_ref[...] += jnp.dot(weights, values, preferred_element_type=jnp.float32)
        return carry

    lax.fori_loop(0, key_count // block, step, 0, unroll=True)


def attend_kernel(q_ref, k_ref, v_ref, *refs, head_size, finish):
    acc_ref = refs[-1]
    rows, lanes = q_ref.shape
    fold_keys(
        stack_heads(q_ref[...], head_size),
        lambda r: k_ref[r, :],
        lambda r: v_ref[r, :],
        acc_ref,
        k_ref.shape[0],
        lanes,
    )
    mixed, totals = pick_heads(acc_ref, rows, lanes, head_size)
    if finish:
        refs[0][...] = (mixed / totals).astype(jnp.bfloat16)
    else:
        refs[0][...] = mixed.astype(jnp.bfloat16)
        refs[1][...] = totals


def attend(queries, kv, head_size, finish):
    count, width = queries.shape
    keys = kv.shape[0]
    lanes = min(128, width)
    pairs = width // lanes
    block = math.gcd(count, 512)
    outs = [jax.ShapeDtypeStruct((count, width), jnp.bfloat16)]
    if not finish:
        outs.append(jax.ShapeDtypeStruct((count, width), jnp.float32))
    if width % 128:
        keys_values = (kv[:, :width], kv[:, width:])
        shift = 0
    else:
        keys_values = (kv, kv)
        shift = pairs
    result = pl.pallas_call(
        functools.partial(attend_kernel, head_size=head_size, finish=finish),
        out_shape=outs,
        grid=(pairs, count // block),
        in_specs=[
            pl.BlockSpec((block, lanes), lambda p, i: (i, p)),
            pl.BlockSpec((keys, lanes), lambda p, i: (0, p)),
            pl.BlockSpec((keys, lanes), lambda p, i: (0, p + shift)),
        ],
        out_specs=[pl.BlockSpec((block, lanes), lambda p, i: (i, p))] * len(outs),
        scratch_shapes=[pltpu.VMEM((lanes // head_size * block, 2 * lanes), jnp.float32)],
        compiler_params=pltpu.CompilerParams(vmem_limit_bytes=VMEM_LIMIT),
        cost_estimate=pl.CostEstimate(
            flops=16 * count * keys * width,
            bytes_accessed=2 * (3 * count * width + 2 * keys * width),
            transcendentals=count * keys * width // head_size,
        ),
    )(queries, *keys_values)
    return result


def per_device(
    tri_tokens, image_tokens, cross_q, cross_kv, cross_out, self_qkv, self_out, mlp_in, mlp_out,
    *, tok
):
    width = cross_q.shape[1]
    head_size = tri_tokens.shape[1] // HEADS
    head_count = width // head_size
    query_factor = score_gain / math.sqrt(head_size) * math.log2(math.e)

    def spread(stream):
        return lax.all_gather(layer_norm(stream).astype(jnp.bfloat16), "head", axis=0, tiled=True)

    def collect(operand, weight):
        return lax.psum_scatter(
            jnp.dot(operand, weight, preferred_element_type=jnp.float32).astype(jnp.bfloat16),
            "head",
            scatter_dimension=0,
            tiled=True,
        ).astype(jnp.float32)

    stream_zero = tri_tokens.astype(jnp.float32)
    (queries,) = project(spread(stream_zero), cross_q[None], ((0, 0, query_factor),), head_size)
    (view_kv,) = project(image_tokens, cross_kv, ((0, 0, 1.0), (0, 1, None)), head_size)
    all_queries = lax.all_gather(queries, "tok", axis=0, tiled=True)
    weighted, totals = attend(all_queries, view_kv, head_size, False)
    group = queries.shape[0]
    totals = totals.reshape(tok, group, head_count, head_size)[:, :, :, 0]
    totals = totals.transpose(0, 2, 1).astype(jnp.bfloat16)
    weighted = lax.psum_scatter(weighted, "tok", scatter_dimension=0, tiled=True)
    totals = lax.psum_scatter(totals, "tok", scatter_dimension=0, tiled=True)
    totals = jnp.repeat(totals[0].T.astype(jnp.float32), head_size, axis=1)
    mix = (weighted.astype(jnp.float32) / totals).astype(jnp.bfloat16)
    stream_one = stream_zero + collect(mix, cross_out)
    self_queries, self_kv = project(
        spread(stream_one), self_qkv, ((0, 0, query_factor), (1, 0, 1.0), (1, 1, None)), head_size
    )
    all_kv = lax.all_gather(self_kv, "tok", axis=0, tiled=True)
    (mix,) = attend(self_queries, all_kv, head_size, True)
    stream_two = stream_one + collect(mix, self_out)
    hidden = jax.nn.gelu(
        jnp.dot(spread(stream_two), mlp_in, preferred_element_type=jnp.float32), approximate=True
    ).astype(jnp.bfloat16)
    return (stream_two + collect(hidden, mlp_out)).astype(jnp.bfloat16)


def solution(mesh):
    return jax.shard_map(
        functools.partial(per_device, tok=mesh.shape["tok"]),
        mesh=mesh,
        in_specs=(
            P(("tok", "head"), None),
            P("tok", None),
            P(None, "head"),
            P(None, None, "head"),
            P("head", None),
            P(None, None, "head"),
            P("head", None),
            P(None, "head"),
            P("head", None),
        ),
        out_specs=P(("tok", "head"), None),
        check_vma=False,
    )
```
